512 devices in a mesh: row: 128 (over z, x, core), col: 4 (over y).
Axes of the slice: x: 4, y: 4, z: 16, core: 2. Of those that a mesh axis runs over, the one named last changes fastest.
Arguments:
- panels: float32 [2, 46, 2048, 2048], P(None, None, 'row', 'col'), may hold values from -0.01953125 to 0.01953125
- coupling: float32 [2048, 2048], P('row', 'col'), may hold values from -0.01953125 to 0.01953125
- diag_inverse: float32 [2, 2048, 2048], P(None, 'row', 'col'), as said below
- rhs: float32 [2, 2048, 512], P(None, 'col', 'row'), may hold values from -6 to 6
- solved: float32 [46, 2048, 512], P(None, 'row', 'col'), may hold values from -6 to 6
- pivot_order: int32 [4096], replicated, may hold values from 0 to 4095, each once
Outputs:
- unknowns: float32 [2, 2048, 512], P(None, 'row', 'col')
The draws below stay inside these ranges and needn't reach their ends.
Inputs may be any that keep to these rules, and one draw needn't show every extreme that they name: diag_inverse is upper triangular with ones on its diagonal. `pivot_order`: every row of the window is named once.
All inputs are finite; a program needn't handle non-finite values.
Results may differ from the reference program's by a relative error of at most 0.0001.
Values sent between devices are 32-bit elements; how exact they have to be, the bound alone decides.
No kernel may reach another device: no remote copies, remote signals or barrier semaphores. Data moves between devices by JAX's collectives and lax.ppermute only.
A program may use at most 64 MiB of HBM per device.

```python
import math
import jax
import jax.numpy as jnp
from jax import lax

NB = 2048
RHS = 512
BLOCKS = 48
TAIL = 46


def draw_diag_inverse(key, part):
    rows = lax.broadcasted_iota(jnp.int32, (2, NB, NB), 1)
    cols = lax.broadcasted_iota(jnp.int32, (2, NB, NB), 2)
    values = jax.random.truncated_normal(key, -3.0, 3.0, (2, NB, NB), jnp.float32)
    above = jnp.where(cols > rows, values / math.sqrt(NB), 0.0)
    return (above + jnp.where(cols == rows, 1.0, 0.0)).astype(jnp.float32)


def shard_levels(stream_key, dims, cuts, smallest, largest):
    level = 1.0
    for dim, shards_of in cuts:
        steps = jax.random.uniform(jax.random.fold_in(jax.random.fold_in(stream_key, 6), dim), (shards_of,), jnp.float32, smallest / len(cuts), largest / len(cuts))
        level = level * jnp.repeat(jnp.exp(steps), dims[dim] // shards_of).reshape((-1,) + (1,) * (len(dims) - 1 - dim))
    return level


def scatter_about(rng, dims, scale, limit, pieces=(), kind=jnp.bfloat16):
    result = scale * jax.random.normal(rng, dims, jnp.float32)
    if pieces:
        result = result * shard_levels(rng, dims, pieces, -0.22, 0.18)
    return jnp.clip(result, -limit, limit).astype(kind)


def setup_inputs(seed: int = 0) -> dict:
    key_of = jax.random.split(jax.random.key(seed), 7)
    return {
        "panels": scatter_about(key_of[0], (2, TAIL, NB, NB), (BLOCKS * NB) ** -0.5, 0.01953125, ((2, 128), (3, 4)), jnp.float32),
        "coupling": scatter_about(key_of[1], (NB, NB), (BLOCKS * NB) ** -0.5, 0.01953125, ((0, 128), (1, 4)), jnp.float32),
        "diag_inverse": draw_diag_inverse(jax.random.fold_in(key_of[6], 71), 0),
        "rhs": scatter_about(key_of[3], (2, NB, RHS), 1.0, 6.0, ((1, 4), (2, 128)), jnp.float32),
        "solved": scatter_about(key_of[4], (TAIL, NB, RHS), 1.0, 6.0, ((1, 128), (2, 4)), jnp.float32),
        "pivot_order": jax.random.permutation(key_of[5], 2 * NB).astype(jnp.int32),
    }


def reference(panels, coupling, diag_inverse, rhs, solved, pivot_order):
    highest = lax.Precision.HIGHEST

    def add_block(index, total):
        block = lax.dynamic_index_in_dim(panels, index, 1, keepdims=False)
        values = lax.dynamic_index_in_dim(solved, index, 0, keepdims=False)
        return total + jnp.einsum("kac,ar->kcr", block, values, precision=highest)

    initial = jnp.zeros((2, NB, RHS), jnp.float32)
    sums_tail = lax.fori_loop(0, TAIL, add_block, initial)
    second = jnp.dot(diag_inverse[1], rhs[1] - sums_tail[1], precision=highest)
    carried = sums_tail[0] + jnp.dot(coupling.T, second, precision=highest)
    first = jnp.dot(diag_inverse[0], rhs[0] - carried, precision=highest)
    window = jnp.concatenate([first, second], axis=0)
    return jnp.take(window, pivot_order, axis=0).reshape(2, NB, RHS)
```

```python
import jax
import jax.numpy as jnp
import numpy as np
from jax import lax
from jax.experimental import pallas as pl
from jax.experimental.pallas import tpu as pltpu
from jax.sharding import Mesh
from jax.sharding import PartitionSpec as P

Z, X, C, Y = 16, 4, 2, 4
XC = X * C
ROW = ("z", "x", "c")
F32 = jnp.float32
BF16 = jnp.bfloat16
HIGHEST = lax.Precision.HIGHEST
VMEM = pl.BlockSpec(memory_space=pltpu.VMEM)
SMEM = pl.BlockSpec(memory_space=pltpu.SMEM)


def call(kernel, outs, *args, flops=0, moved=1 << 20):
    specs = [SMEM if a.dtype == jnp.int32 and a.ndim == 1 else VMEM for a in args]
    return pl.pallas_call(
        kernel,
        out_shape=[jax.ShapeDtypeStruct(s, F32) for s in outs],
        in_specs=specs,
        out_specs=[VMEM] * len(outs),
        cost_estimate=pl.CostEstimate(flops=flops, bytes_accessed=moved, transcendentals=0),
        compiler_params=pltpu.CompilerParams(vmem_limit_bytes=48 << 20),
    )(*args)


def exchange(value, axes):
    return lax.all_to_all(value, axes, 0, 0)


def low_lanes(shape):
    return lax.broadcasted_iota(jnp.int32, shape, len(shape) - 1) < 64


def halves(value):
    high = value.astype(BF16)
    return high, (value - high.astype(F32)).astype(BF16)


def tail_kernel(place, s0, s1a, s1b, s2a, s2b, s3a, s3b, panels, rhs, out):
    low = low_lanes((128, 128))
    split = [halves(panels[k]) for k in range(2)]
    for slot in range(4):
        if slot == 0:
            block = s0[...]
        else:
            upper, lower = ((s1a, s1b), (s2a, s2b), (s3a, s3b))[slot - 1]
            block = jnp.concatenate([upper[...], lower[...]], axis=0)
        up, down = halves(jnp.transpose(block))
        sums = []
        for k in range(2):
            high, rest = split[k]
            total = jnp.dot(down, high, preferred_element_type=F32)
            total += jnp.dot(up, rest, preferred_element_type=F32)
            total += jnp.dot(up, high, preferred_element_type=F32)
            sums.append(-total)
        where = place[slot]
        for x in range(X):
            a, b = (s[:, x * 128 : (x + 1) * 128] for s in sums)
            out[0, x, :, where] = jnp.where(low, a, b).reshape(Z, 8, 128)
            out[1, x, :, where] = jnp.where(low, b, a).reshape(Z, 8, 128)
    low = low_lanes((8, 128))
    for x in range(X):
        a, b = (rhs[k, :, x * 128 : (x + 1) * 128] for k in range(2))
        out[0, x, place[4], place[5]] += jnp.where(low, a, b)
        out[1, x, place[4], place[5]] += jnp.where(low, b, a)


def total_of(received):
    total = received[0]
    for i in range(1, received.shape[0]):
        total += received[i]
    return total


def target_kernel(received, out):
    total = total_of(received)
    for i in range(XC):
        out[i] = total


def times_transposed(value, weights):
    return lax.dot_general(
        value, weights, (((1,), (1,)), ((), ())), precision=HIGHEST, preferred_element_type=F32
    )


def gathered_rows(matrices, which):
    return matrices[:, which * 16 : (which + 1) * 16, :].reshape(Z * 16, 512)


def second_kernel(received, matrices, start, out):
    low = low_lanes((32, 128))
    for x in range(X):
        a, b = received[2 * x], received[2 * x + 1]
        start[0, :, x * 128 : (x + 1) * 128] = jnp.where(low, a, b)
        start[1, :, x * 128 : (x + 1) * 128] = jnp.where(low, b, a)
    part = times_transposed(start[1], gathered_rows(matrices, 1))
    for y in range(Y):
        out[y] = part


def carry_kernel(received, matrices, second, out):
    total = total_of(received)
    second[...] = total
    part = jnp.dot(
        total, gathered_rows(matrices, 2), precision=HIGHEST, preferred_element_type=F32
    )
    for i in range(XC):
        out[i] = part


def first_kernel(received, start, matrices, out):
    target = start[0] - total_of(received)
    part = times_transposed(target, gathered_rows(matrices, 0))
    for y in range(Y):
        out[y] = part[y * 8 : (y + 1) * 8, :]


def pick_kernel(place, received, second, chunk, lane, out):
    first = total_of(received)
    at = pl.ds(pl.multiple_of(place[0] * 8, 8), 8)
    parts = [first[:, :128], first[:, 128:], second[at, :128], second[at, 128:]]
    for block in range(32):
        which = jnp.broadcast_to(chunk[block : block + 1, :], (8, 128))
        index = jnp.broadcast_to(lane[block : block + 1, :], (8, 128))
        total = jnp.zeros((8, 128), F32)
        for i in range(4):
            found = jnp.take_along_axis(parts[i], index, axis=1, mode="promise_in_bounds")
            total = jnp.where(which == i, found, total)
        out[block // 4, block % 4] = total


def split_kernel(received, out):
    total = total_of(received)
    for q in range(4):
        for m in range(4):
            out[q * 4 + m] = total[q] if m == 0 else pltpu.roll(total[q], 128 - 32 * m, 1)


def turn_kernel(received, out):
    turned = jnp.transpose(received[...].reshape(128, 128))
    out[0] = turned[0:16]
    out[1] = turned[16:32]


def per_device(panels, coupling, diag_inverse, rhs, solved, pivot_order):
    x, c, y = (lax.axis_index(a) for a in ("x", "c", "y"))
    z = lax.axis_index("z")
    xc = x * C + c
    depth = solved.shape[0] * 16
    half = depth // 2

    own = solved.reshape(depth, 128)
    ring = [(i, (i + 1) % Y) for i in range(Y)]
    back = [(i, (i - 1) % Y) for i in range(Y)]
    below_a = lax.ppermute(own[:half], "y", ring)
    above_b = lax.ppermute(own[half:], "y", back)
    below_b = lax.ppermute(own[half:], "y", ring)
    above_a = lax.ppermute(own[:half], "y", back)
    far_a = lax.ppermute(below_a, "y", ring)
    far_b = lax.ppermute(above_b, "y", back)

    matrices = jnp.concatenate([diag_inverse.reshape(32, 512), coupling], axis=0)
    matrices = lax.all_gather(matrices, "z")

    row = z * XC + xc
    slots = (jnp.arange(8, dtype=jnp.int32) // 4 == row % 2)[None, :, None]
    mine = jnp.transpose(rhs, (0, 2, 1))
    mine = jnp.where(slots, jnp.concatenate([mine, mine], axis=1), 0.0)
    place = jnp.stack(
        [y, (y + 3) % Y, (y + 1) % Y, (y + 2) % Y, (row % 32) // 2, row // 32]
    ).astype(jnp.int32)

    (partial,) = call(
        tail_kernel,
        [(C, X, Z, Y, 8, 128)],
        place,
        own,
        below_a,
        below_b,
        above_a,
        above_b,
        far_a,
        far_b,
        panels.reshape(2, depth, 512),
        mine,
        flops=6 * depth * 512 * 1024,
        moved=7 << 20,
    )
    partial = exchange(partial.reshape(C, X * 512, 128), "c")
    partial = (partial[0] + partial[1]).reshape(X, 512, 128)
    partial = exchange(partial, "x")
    partial = exchange(jnp.sum(partial, axis=0).reshape(Z, 32, 128), "z")

    (part,) = call(target_kernel, [(XC, 32, 128)], partial)
    part = exchange(part, ("x", "c"))
    start, part = call(second_kernel, [(2, 32, 512), (Y, 32, 256)], part, matrices)
    part = exchange(part, "y")
    second, part = call(carry_kernel, [(32, 256), (XC, 32, 512)], part, matrices)
    part = exchange(part, ("x", "c"))
    (part,) = call(first_kernel, [(Y, 8, 256)], part, start, matrices)
    part = exchange(part, "y")

    sources = jnp.transpose(pivot_order.reshape(2, Z, XC, 16), (2, 1, 0, 3)).reshape(32, 128)
    order = (sources >> 7) & 15
    chunk = jnp.where(((sources >> 4) & 7) == xc, ((sources >> 11) & 1) * 2 + (order >> 3), 4)
    lane = (order & 7) * 16 + (sources & 15)
    (part,) = call(pick_kernel, [(XC, 4, 8, 128)], place, part, second, chunk, lane)
    part = exchange(part, ("x", "c"))
    (part,) = call(split_kernel, [(Z, 8, 128)], part)
    part = exchange(part, "z")
    (unknowns,) = call(turn_kernel, [(2, 16, 128)], part)
    return unknowns


def solution(mesh):
    wide = Mesh(np.asarray(mesh.devices).reshape(Z, X, C, Y), ("z", "x", "c", "y"))
    in_specs = (
        P(None, None, ROW, "y"),
        P(ROW, "y"),
        P(None, ROW, "y"),
        P(None, "y", ROW),
        P(None, ROW, "y"),
        P(),
    )
    return jax.shard_map(
        per_device, mesh=wide, in_specs=in_specs, out_specs=P(None, ROW, "y"), check_vma=False
    )
```

```python
import jax
import jax.numpy as jnp
import numpy as np
from jax import lax
from jax.experimental import pallas as pl
from jax.experimental.pallas import tpu as pltpu
from jax.sharding import Mesh
from jax.sharding import PartitionSpec as P

Z, X, C, Y = 16, 4, 2, 4
XC = X * C
ROW = ("z", "x", "c")
F32 = jnp.float32
BF16 = jnp.bfloat16
HIGHEST = lax.Precision.HIGHEST
VMEM = pl.BlockSpec(memory_space=pltpu.VMEM)
SMEM = pl.BlockSpec(memory_space=pltpu.SMEM)


def call(kernel, outs, *args, flops=0, moved=1 << 20):
    specs = [SMEM if a.dtype == jnp.int32 and a.ndim == 1 else VMEM for a in args]
    return pl.pallas_call(
        kernel,
        out_shape=[
            jax.ShapeDtypeStruct(*s) if isinstance(s[0], tuple) else jax.ShapeDtypeStruct(s, F32)
            for s in outs
        ],
        in_specs=specs,
        out_specs=[VMEM] * len(outs),
        cost_estimate=pl.CostEstimate(flops=flops, bytes_accessed=moved, transcendentals=0),
        compiler_params=pltpu.CompilerParams(vmem_limit_bytes=20 << 20),
    )(*args)


def exchange(value, axes):
    return lax.all_to_all(value, axes, 0, 0)


def low_lanes(shape):
    return lax.broadcasted_iota(jnp.int32, shape, len(shape) - 1) < 64


def halves(value):
    high = value.astype(BF16)
    return high, (value - high.astype(F32)).astype(BF16)


def products(block, highs, rests, outs):
    low = low_lanes((128, 128))
    up, down = halves(jnp.transpose(block))
    sums = []
    for k in range(2):
        high, rest = highs[k], rests[k]
        total = jnp.dot(down, high, preferred_element_type=F32)
        total += jnp.dot(up, rest, preferred_element_type=F32)
        total += jnp.dot(up, high, preferred_element_type=F32)
        sums.append(-total)
    for x in range(X):
        a, b = (s[:, x * 128 : (x + 1) * 128] for s in sums)
        outs(0, x, jnp.where(low, a, b).reshape(Z, 8, 128))
        outs(1, x, jnp.where(low, b, a).reshape(Z, 8, 128))


def own_kernel(block, panels, part, highs, rests):
    for k in range(2):
        highs[k], rests[k] = halves(panels[k])

    def put(c, x, value):
        part[c, x] = value

    products(block[...], highs, rests, put)


def next_kernel(near, other, highs, rests, part_1, part_2):
    for block, part in ((near, part_1), (other, part_2)):

        def put(c, x, value):
            part[c, x] = value

        products(block[...], highs, rests, put)


def tail_kernel(place, far, highs, rests, part_0, part_1, part_2, rhs, out):
    def put(c, x, value):
        out[c, x, :, place[3]] = value

    products(far[...], highs, rests, put)
    for slot, part in enumerate((part_0, part_1, part_2)):
        for c in range(C):
            for x in range(X):
                out[c, x, :, place[slot]] = part[c, x]
    low = low_lanes((8, 128))
    for x in range(X):
        a, b = (rhs[k, :, x * 128 : (x + 1) * 128] for k in range(2))
        out[0, x, place[4], place[5]] += jnp.where(low, a, b)
        out[1, x, place[4], place[5]] += jnp.where(low, b, a)


def total_of(received):
    total = received[0]
    for i in range(1, received.shape[0]):
        total += received[i]
    return total


def target_kernel(place, received, target, out):
    total = total_of(received)
    target[...] = total
    valid = low_lanes((16, 128)) == (place[6] == 1)
    packed = jnp.where(valid, total[:16], pltpu.roll(total[16:], 64, 1))
    for i in range(XC):
        out[i] = packed


def times_transposed(value, weights):
    return lax.dot_general(
        value, weights, (((1,), (1,)), ((), ())), precision=HIGHEST, preferred_element_type=F32
    )


def gathered_rows(matrices, which):
    return matrices[:, which * 16 : (which + 1) * 16, :].reshape(Z * 16, 512)


def second_kernel(received, matrices, out):
    low = low_lanes((16, 128))
    columns = []
    for x in range(X):
        a, b = received[2 * x], received[2 * x + 1]
        upper = jnp.where(low, b, a)
        lower = pltpu.roll(jnp.where(low, a, b), 64, 1)
        columns.append(jnp.concatenate([upper, lower], axis=0))
    part = times_transposed(jnp.concatenate(columns, axis=1), gathered_rows(matrices, 1))
    for y in range(Y):
        out[y] = part


def carry_kernel(place, received, target, matrices, second, out):
    total = total_of(received)
    second[...] = total
    part = jnp.dot(
        total, gathered_rows(matrices, 2), precision=HIGHEST, preferred_element_type=F32
    )
    valid = low_lanes((32, 128)) == (place[6] == 0)
    mine = jnp.where(valid, target[...], 0.0)
    for x in range(X):
        piece = jnp.where(place[7] == x, mine, 0.0) - part[:, x * 128 : (x + 1) * 128]
        for i in range(XC):
            out[i, :, x * 128 : (x + 1) * 128] = piece


def first_kernel(received, matrices, out):
    part = times_transposed(total_of(received), gathered_rows(matrices, 0))
    for y in range(Y):
        out[y] = part[y * 8 : (y + 1) * 8, :]


def pick_kernel(place, received, second, chunk, lane, out):
    first = total_of(received)
    at = pl.ds(pl.multiple_of(place[0] * 8, 8), 8)
    parts = [first[:, :128], first[:, 128:], second[at, :128], second[at, 128:]]
    for block in range(32):
        which = jnp.broadcast_to(chunk[block : block + 1, :], (8, 128))
        index = jnp.broadcast_to(lane[block : block + 1, :], (8, 128))
        total = jnp.zeros((8, 128), F32)
        for i in range(4):
            found = jnp.take_along_axis(parts[i], index, axis=1, mode="promise_in_bounds")
            total = jnp.where(which == i, found, total)
        out[block // 4, block % 4] = total


def split_kernel(received, out):
    total = total_of(received)
    for q in range(4):
        for m in range(4):
            out[q * 4 + m] = total[q] if m == 0 else pltpu.roll(total[q], 128 - 32 * m, 1)


def turn_kernel(received, out):
    turned = jnp.transpose(received[...].reshape(128, 128))
    out[0] = turned[0:16]
    out[1] = turned[16:32]


def per_device(panels, coupling, diag_inverse, rhs, solved, pivot_order):
    x, c, y = (lax.axis_index(a) for a in ("x", "c", "y"))
    z = lax.axis_index("z")
    xc = x * C + c
    depth = solved.shape[0] * 16

    own = solved.reshape(depth, 128)
    pairs = [(i // Y, i % Y) for i in range(C * Y)]
    turn = [(i * Y + j, i * Y + (j + 1 - 2 * i) % Y) for i, j in pairs]
    back = [(there, here) for here, there in turn]
    near = lax.ppermute(own, ("c", "y"), turn)
    matrices = jnp.concatenate([diag_inverse.reshape(32, 512), coupling], axis=0)
    matrices = lax.all_gather(matrices, "z")
    other = lax.ppermute(own, ("c", "y"), back)
    far = lax.ppermute(near, ("c", "y"), turn)

    row = z * XC + xc
    slots = (jnp.arange(8, dtype=jnp.int32) // 4 == row % 2)[None, :, None]
    mine = jnp.transpose(rhs, (0, 2, 1))
    mine = jnp.where(slots, jnp.concatenate([mine, mine], axis=1), 0.0)
    place = jnp.stack(
        [y, (y + 3 - 2 * c) % Y, (y + 1 + 2 * c) % Y, (y + 2) % Y, (row % 32) // 2, row // 32, c, x]
    ).astype(jnp.int32)

    piece = (C, X, Z, 8, 128)
    split = ((2, depth, 512), BF16)
    work = 6 * depth * 128 * 1024
    part_0, highs, rests = call(
        own_kernel, [piece, split, split], own, panels.reshape(2, depth, 512), flops=work
    )
    part_1, part_2 = call(
        next_kernel, [piece, piece], near, other, highs, rests, flops=2 * work
    )
    (partial,) = call(
        tail_kernel,
        [(C, X, Z, Y, 8, 128)],
        place,
        far,
        highs,
        rests,
        part_0,
        part_1,
        part_2,
        mine,
        flops=work,
    )
    partial = exchange(partial.reshape(C, X * 512, 128), "c")
    partial = (partial[0] + partial[1]).reshape(X, 512, 128)
    partial = exchange(partial, "x")
    partial = exchange(jnp.sum(partial, axis=0).reshape(Z, 32, 128), "z")

    target, part = call(target_kernel, [(32, 128), (XC, 16, 128)], place, partial)
    part = exchange(part, ("x", "c"))
    (part,) = call(second_kernel, [(Y, 32, 256)], part, matrices)
    part = exchange(part, "y")
    second, part = call(
        carry_kernel, [(32, 256), (XC, 32, 512)], place, part, target, matrices
    )
    part = exchange(part, ("x", "c"))
    (part,) = call(first_kernel, [(Y, 8, 256)], part, matrices)
    part = exchange(part, "y")

    sources = jnp.transpose(pivot_order.reshape(2, Z, XC, 16), (2, 1, 0, 3)).reshape(32, 128)
    order = (sources >> 7) & 15
    chunk = jnp.where(((sources >> 4) & 7) == xc, ((sources >> 11) & 1) * 2 + (order >> 3), 4)
    lane = (order & 7) * 16 + (sources & 15)
    (part,) = call(pick_kernel, [(XC, 4, 8, 128)], place, part, second, chunk, lane)
    part = exchange(part, ("x", "c"))
    (part,) = call(split_kernel, [(Z, 8, 128)], part)
    part = exchange(part, "z")
    (unknowns,) = call(turn_kernel, [(2, 16, 128)], part)
    return unknowns


def solution(mesh):
    wide = Mesh(np.asarray(mesh.devices).reshape(Z, X, C, Y), ("z", "x", "c", "y"))
    in_specs = (
        P(None, None, ROW, "y"),
        P(ROW, "y"),
        P(None, ROW, "y"),
        P(None, "y", ROW),
        P(None, ROW, "y"),
        P(),
    )
    return jax.shard_map(
        per_device, mesh=wide, in_specs=in_specs, out_specs=P(None, ROW, "y"), check_vma=False
    )
```
